512 devices in a mesh: row: 32 (over x, y, core), pair: 16 (over z).
Axes of the slice: x: 4, y: 4, z: 16, core: 2. Of those that a mesh axis runs over, the one named last changes fastest.
Arguments:
- matrix: float32 [65536, 2048], P('row', 'pair'), may hold values from -80 to 80
- partner: int32 [3, 16], replicated, may hold values from 0 to 15, as said below
Outputs:
- result: float32 [65536, 2048], P('row', 'pair')
The draws below stay inside these ranges and needn't reach their ends.
Inputs may be any that keep to these rules, and one draw needn't show every extreme that they name: partner[r, j] equals j XOR s_r, where s_r is a power of two below 16 and the same for every j of round r.
All inputs are finite; a program needn't handle non-finite values.
Results may differ from the reference program's by a relative error of at most 0.0003.
Values sent between devices are 32-bit elements; how exact they have to be, the bound alone decides.
A program may use at most 64 MiB of HBM per device.

```python
import math
import jax
import jax.numpy as jnp
from jax import lax

B = 64
ROUNDS = 4
NS_ITERS = 6
ROWS = 65536
COLS = 2048
N_PAIR = 16


def draw_matrix(key, part):
    key_row, key_col, key_base = jax.random.split(key, 3)
    ramp = 1.0 + 2.0 * jnp.arange(ROWS, dtype=jnp.float32) / (ROWS - 1)
    rough_row = jnp.exp(jax.random.uniform(key_row, (ROWS,), jnp.float32, 0.0, math.log(4.0)))
    column_scale = jnp.exp(jax.random.uniform(key_col, (COLS,), jnp.float32, 0.0, math.log(10.0)))
    base = jnp.clip(jax.random.normal(key_base, (ROWS, COLS), jnp.float32), -6.0, 6.0)
    return (0.1 * base * (ramp * rough_row)[:, None] * column_scale[None, :]).astype(jnp.float32)


def draw_partner(key, part):
    bit_total = N_PAIR.bit_length() - 1
    bits = jax.random.randint(key, (ROUNDS - 1,), 0, bit_total, dtype=jnp.int32)
    offsets = jnp.left_shift(jnp.ones((ROUNDS - 1,), jnp.int32), bits)
    return jnp.bitwise_xor(jnp.arange(N_PAIR, dtype=jnp.int32)[None, :], offsets[:, None]).astype(jnp.int32)


def setup_inputs(seed: int = 0) -> dict:
    seeds = jax.random.split(jax.random.key(seed), 3)
    matrix = draw_matrix(jax.random.fold_in(seeds[2], 71), 0)
    partner = draw_partner(jax.random.fold_in(seeds[2], 71), 0)
    return {"matrix": matrix, "partner": partner}


def orthogonalizer(gram):
    identity = jnp.eye(gram.shape[0], dtype=jnp.float32)
    frobenius = jnp.sqrt(jnp.sum(gram * gram))
    square_root = gram / frobenius
    inverse_root = identity
    for step_count in range(NS_ITERS):
        correction = 1.5 * identity - 0.5 * jnp.dot(inverse_root, square_root, precision=lax.Precision.HIGHEST)
        square_root = jnp.dot(square_root, correction, precision=lax.Precision.HIGHEST)
        inverse_root = jnp.dot(correction, inverse_root, precision=lax.Precision.HIGHEST)
    return inverse_root * (jnp.sqrt(jnp.diagonal(gram)) / jnp.sqrt(frobenius))[None, :]

def reference(matrix, partner):
    blocks = matrix.reshape(ROWS, N_PAIR, 2 * B).transpose(1, 0, 2)
    for round_index in range(ROUNDS):
        gram = jnp.einsum('prc,prd->pcd', blocks, blocks, precision=lax.Precision.HIGHEST)
        rotation = jax.vmap(orthogonalizer)(gram)
        blocks = jnp.einsum('prc,pcd->prd', blocks, rotation, precision=lax.Precision.HIGHEST)
        if round_index + 1 < ROUNDS:
            second = blocks[:, :, B:][partner[round_index]]
            blocks = jnp.concatenate([blocks[:, :, :B], second], axis=2)
    return blocks.transpose(1, 0, 2).reshape(ROWS, 2 * B * N_PAIR)
```

```python
import functools

import jax
import jax.numpy as jnp
from jax import lax
from jax.experimental import pallas as pl
from jax.experimental.pallas import tpu as pltpu
from jax.sharding import PartitionSpec as P

ROUNDS = 4
NS_ITERS = 6
MESH = pl.DeviceIdType.MESH
HIGHEST = lax.Precision.HIGHEST


def dot(a, b):
    return jnp.dot(a, b, precision=HIGHEST, preferred_element_type=jnp.float32)


def orthogonalizer(gram):
    size = gram.shape[0]
    rows = lax.broadcasted_iota(jnp.int32, (size, size), 0)
    cols = lax.broadcasted_iota(jnp.int32, (size, size), 1)
    identity = jnp.where(rows == cols, 1.0, 0.0).astype(jnp.float32)
    square_sum = jnp.sum(jnp.sum(gram * gram, axis=0, keepdims=True), axis=1, keepdims=True)
    frobenius = jnp.sqrt(square_sum)
    root = gram / frobenius
    inverse = 1.5 * identity - 0.5 * root
    root = dot(root, inverse)
    for step in range(1, NS_ITERS):
        correction = 1.5 * identity - 0.5 * dot(inverse, root)
        if step + 1 < NS_ITERS:
            root = dot(root, correction)
        inverse = dot(correction, inverse)
    diagonal = jnp.sum(gram * identity, axis=0, keepdims=True)
    return inverse * (jnp.sqrt(diagonal) / jnp.sqrt(frobenius))


def transform_kernel(gram_ref, v_ref, half, mid, full, core_slot, y_slot, x_slot, send, recv):
    row, z = lax.axis_index("row"), lax.axis_index("pair")
    core = lax.rem(row, 2)
    y = lax.rem(lax.div(row, 2), 4)
    x = lax.div(row, 8)
    other = row + 1 - 2 * core
    y_peers = [x * 8 + lax.rem(y + k, 4) * 2 + core for k in (1, 2, 3)]
    x_peers = [lax.rem(x + k, 4) * 8 + y * 2 + core for k in (1, 2, 3)]
    barrier = pltpu.get_barrier_semaphore()
    for peer in [other] + y_peers + x_peers:
        pl.semaphore_signal(barrier, inc=1, device_id=(peer, z), device_id_type=MESH)
    pl.semaphore_wait(barrier, 7)

    h = gram_ref.shape[0] // 2
    mine = pl.ds(pl.multiple_of(core * h, h), h)
    theirs = pl.ds(pl.multiple_of((1 - core) * h, h), h)

    def copy(src, dst, slot, peer):
        return pltpu.make_async_remote_copy(
            src_ref=src, dst_ref=dst, send_sem=send.at[slot], recv_sem=recv.at[slot],
            device_id=(peer, z), device_id_type=MESH,
        )

    first = copy(gram_ref.at[theirs], core_slot, 0, other)
    first.start()
    first.wait_recv()
    half[...] = gram_ref[mine] + core_slot[...]
    y_copies = [copy(half, y_slot.at[k], 1 + k, y_peers[k]) for k in range(3)]
    for c in y_copies:
        c.start()
    total = half[...]
    for k, c in enumerate(y_copies):
        c.wait_recv()
        total = total + y_slot[k]
    mid[...] = total
    x_copies = [copy(mid, x_slot.at[k], 4 + k, x_peers[k]) for k in range(3)]
    for c in x_copies:
        c.start()
    for k, c in enumerate(x_copies):
        c.wait_recv()
        total = total + x_slot[k]
    full[mine] = total
    last = copy(full.at[mine], full.at[mine], 7, other)
    last.start()
    last.wait_recv()
    v_ref[...] = orthogonalizer(full[...])
    for c in [first] + y_copies + x_copies + [last]:
        c.wait_send()


def transform(gram):
    n = gram.shape[0]
    h = n // 2
    vmem = pl.BlockSpec(memory_space=pltpu.VMEM)
    return pl.pallas_call(
        transform_kernel,
        out_shape=jax.ShapeDtypeStruct((n, n), jnp.float32),
        in_specs=[vmem],
        out_specs=vmem,
        scratch_shapes=[
            pltpu.VMEM((h, n), jnp.float32),
            pltpu.VMEM((h, n), jnp.float32),
            pltpu.VMEM((n, n), jnp.float32),
            pltpu.VMEM((h, n), jnp.float32),
            pltpu.VMEM((3, h, n), jnp.float32),
            pltpu.VMEM((3, h, n), jnp.float32),
            pltpu.SemaphoreType.DMA((8,)),
            pltpu.SemaphoreType.DMA((8,)),
        ],
        compiler_params=pltpu.CompilerParams(collective_id=0, has_side_effects=True),
        name="transform",
    )(gram)


def partner_2(value, axis, stride):
    mask = 2**stride
    pairs = [(source, source ^ mask) for source in range(lax.axis_size(axis))]
    return lax.ppermute(value, axis, pairs)


def swap_branch(bit_index):
    def apply_swap(folded):
        return partner_2(folded, "pair", bit_index)

    return apply_swap


def body(matrix, partner):
    rows_here, width = matrix.shape
    half_width = width // 2
    pair_count = lax.axis_size("pair")
    bit_total = pair_count.bit_length() - 1
    my_pair = lax.axis_index("pair")
    columns = matrix
    for round_index in range(ROUNDS):
        rotation = transform(dot(columns.T, columns))
        columns = dot(columns, rotation)
        if round_index + 1 < ROUNDS:
            offset = jnp.bitwise_xor(partner[round_index, my_pair], my_pair)
            folded = columns[:, half_width:].reshape(rows_here // 2, width)
            positions = jnp.arange(bit_total, dtype=jnp.int32)
            which_bit = jnp.sum(jnp.bitwise_and(jnp.right_shift(offset, positions), 1) * positions)
            folded = lax.switch(
                which_bit, [swap_branch(bit_index) for bit_index in range(bit_total)], folded
            )
            second = folded.reshape(rows_here, half_width)
            columns = jnp.concatenate([columns[:, :half_width], second], axis=1)
    return columns


def solution(mesh):
    in_specs = (P("row", "pair"), P())
    out_specs = P("row", "pair")
    return jax.shard_map(body, mesh=mesh, in_specs=in_specs, out_specs=out_specs, check_vma=False)
```

```python
import functools

import jax
import jax.numpy as jnp
from jax import lax
from jax.experimental import pallas as pl
from jax.experimental.pallas import tpu as pltpu
from jax.sharding import PartitionSpec as P

ROUNDS = 4
NS_ITERS = 6
CHUNKS = 8
MESH = pl.DeviceIdType.MESH
HIGHEST = lax.Precision.HIGHEST
F32 = jnp.float32

OFFSETS = sorted(
    [(dx, dy) for dx in range(4) for dy in range(4) if dx or dy],
    key=lambda d: -(min(d[0], 4 - d[0]) + min(d[1], 4 - d[1])),
)


def dot(a, b):
    return jnp.dot(a, b, precision=HIGHEST, preferred_element_type=F32)


def dot_t(a, b):
    return lax.dot_general(
        a, b, (((0,), (0,)), ((), ())), precision=HIGHEST, preferred_element_type=F32
    )


def low_lanes(shape, half):
    return lax.broadcasted_iota(jnp.int32, shape, 1) < half


def orthogonalizer(gram, both, corr):
    size = gram.shape[0]
    rows = lax.broadcasted_iota(jnp.int32, (size, size), 0)
    cols = lax.broadcasted_iota(jnp.int32, (size, size), 1)
    identity = jnp.where(rows == cols, 1.0, 0.0).astype(F32)
    square_sum = jnp.sum(jnp.sum(gram * gram, axis=0, keepdims=True), axis=1, keepdims=True)
    frobenius = jnp.sqrt(square_sum)
    root = gram / frobenius
    inverse = 1.5 * identity - 0.5 * root
    root = dot(root, inverse)

    both[:size] = root
    both[size:] = inverse

    def step(_, carry):
        corr[...] = 1.5 * identity - 0.5 * dot(both[size:], both[:size])
        both[...] = dot(both[...], corr[...])
        return carry

    lax.fori_loop(0, NS_ITERS - 2, step, 0)
    inverse = dot(both[size:], 1.5 * identity - 0.5 * dot(both[size:], both[:size]))
    diagonal = jnp.sum(gram * identity, axis=0, keepdims=True)
    return inverse * (jnp.sqrt(diagonal) / jnp.sqrt(frobenius))


def diagonal_blocks(gram_e, gram_s):
    h = gram_e.shape[0] // 2
    low = low_lanes((h, 2 * h), h)
    a = jnp.where(low, gram_e[:h], gram_e[h:])
    b = jnp.where(low, gram_s[:h], gram_s[h:])
    a = a + pltpu.roll(a, h, 1)
    b = b + pltpu.roll(b, h, 1)
    return jnp.where(low, a, b)


def cross_block(product):
    h = product.shape[0] // 2
    c = jnp.where(low_lanes((h, 2 * h), h), product[h:], product[:h])
    c = c + pltpu.roll(c, h, 1)
    q = h // 2
    return jnp.where(low_lanes((q, 2 * h), h), c[:q], c[q:])


def assemble(diagonal, cross):
    h = diagonal.shape[0]
    low = low_lanes((h, 2 * h), h)
    zero = jnp.zeros((h, 2 * h), F32)
    c = jnp.concatenate([pltpu.roll(cross, h, 1), cross], axis=0)
    upper = jnp.concatenate([jnp.where(low, 0.0, c), zero], axis=0)
    blocks = jnp.concatenate(
        [jnp.where(low, diagonal, 0.0), jnp.where(low, 0.0, diagonal)], axis=0
    )
    return blocks + upper + upper.T


class Place:
    def __init__(self):
        self.row, self.z = lax.axis_index("row"), lax.axis_index("pair")
        self.core = lax.rem(self.row, 2)
        y = lax.rem(lax.div(self.row, 2), 4)
        x = lax.div(self.row, 8)
        self.other = self.row + 1 - 2 * self.core
        self.peers = [
            (lax.rem(x + dx, 4) * 4 + lax.rem(y + dy, 4)) * 2 + self.core for dx, dy in OFFSETS
        ]

    def greet(self, more=()):
        barrier = pltpu.get_barrier_semaphore()
        targets = [(r, self.z) for r in self.peers + [self.other]] + [(self.row, p) for p in more]
        for target in targets:
            pl.semaphore_signal(barrier, inc=1, device_id=target, device_id_type=MESH)
        return lambda: pl.semaphore_wait(barrier, len(targets))

    def half(self, ref_rows):
        h = ref_rows // 2
        return (
            pl.ds(pl.multiple_of(self.core * h, h), h),
            pl.ds(pl.multiple_of((1 - self.core) * h, h), h),
        )


def copy(src, dst, send, recv, target):
    return pltpu.make_async_remote_copy(
        src_ref=src, dst_ref=dst, send_sem=send, recv_sem=recv,
        device_id=target, device_id_type=MESH,
    )


def exchange(place, src, slots, send, recv, base):
    copies = [
        copy(src, slots.at[k], send.at[base + k], recv.at[base + k], (peer, place.z))
        for k, peer in enumerate(place.peers)
    ]
    for c in copies:
        c.start()
    return copies


def collect(copies, slots, total):
    for k in reversed(range(len(copies))):
        copies[k].wait_recv()
        total = total + slots[k]
    return total


def split_sum(place, local, half, slot, slots, result, send, recv, base):
    mine, theirs = place.half(local.shape[0])
    first = copy(local.at[theirs], slot, send.at[base], recv.at[base], (place.other, place.z))
    first.start()
    first.wait_recv()
    half[...] = local[mine] + slot[...]
    copies = exchange(place, half, slots, send, recv, base + 1)
    result[mine] = collect(copies, slots, half[...])
    last = copy(
        result.at[mine], result.at[mine], send.at[base + 16], recv.at[base + 16],
        (place.other, place.z),
    )
    last.start()
    last.wait_recv()
    return [first] + copies + [last]


def start_kernel(x_ref, e_ref, s_ref, g_ref, local, half, slot, slots, result, send, recv):
    place = Place()
    wait = place.greet()
    n, w = x_ref.shape
    n, h = n // 2, w // 2
    m = n // 4
    low = low_lanes((m, w), h)

    def square(c, grams):
        rows = pl.ds(pl.multiple_of(c * m, m), m)
        top = x_ref[rows]
        bottom = pltpu.roll(x_ref[pl.ds(pl.multiple_of(n + c * m, m), m)], h, 1)
        e, s = jnp.where(low, top, bottom), jnp.where(low, bottom, top)
        e_ref[rows] = e
        s_ref[rows] = s
        return grams[0] + dot_t(e, e), grams[1] + dot_t(s, s), grams[2] + dot_t(e, s)

    zero = jnp.zeros((w, w), F32)
    ee, ss, es = lax.fori_loop(0, 4, square, (zero, zero, zero))
    local[:h] = diagonal_blocks(ee, ss)
    local[h:] = cross_block(es)
    wait()
    copies = split_sum(place, local, half, slot, slots, result, send, recv, 0)
    g_ref[...] = assemble(result[:h], result[h:])
    for c in copies:
        c.wait_send()


def block_form(v):
    h = v.shape[0] // 2
    low = low_lanes((h, 2 * h), h)
    va, vb = v[:h], v[h:]
    ra, rb = pltpu.roll(va, h, 1), pltpu.roll(vb, h, 1)
    left = [jnp.where(low, va, 0.0), jnp.where(low, 0.0, ra), jnp.where(low, 0.0, rb), jnp.where(low, vb, 0.0)]
    right = [jnp.where(low, 0.0, va), jnp.where(low, ra, 0.0), jnp.where(low, rb, 0.0), jnp.where(low, 0.0, vb)]
    return jnp.concatenate(
        [jnp.concatenate(left, axis=0), jnp.concatenate(right, axis=0)], axis=1
    )


def round_kernel(
    stride, p_ref, q_ref, g_ref, e_ref, r_ref, gout_ref,
    s_ref, w_ref, dlocal, dhalf, dslot, dslots, dresult, dother, clocal, cslot, csum, cslots,
    bsend, brecv, send, recv, both, corr,
):
    place = Place()
    bit = lax.rem(lax.div(place.z, stride), 2)
    partner = place.z + stride * (1 - 2 * bit)
    wait = place.greet([partner])
    n, w = p_ref.shape
    h, m = w // 2, n // CHUNKS
    across = (place.row, partner)

    w_ref[...] = block_form(orthogonalizer(g_ref[...], both, corr))
    wait()

    def bulk(c):
        rows = pl.ds(pl.multiple_of(c * m, m), m)
        return rows, copy(s_ref.at[rows], r_ref.at[rows], bsend.at[c], brecv.at[c], across)

    def give(c, _):
        rows, out = bulk(c)
        es = dot(jnp.concatenate([p_ref[rows], q_ref[rows]], axis=1), w_ref[...])
        s_ref[rows] = es[:, w:]
        out.start()
        e_ref[rows] = es[:, :w]
        return 0

    lax.fori_loop(0, CHUNKS, give, 0)

    def square(c, grams):
        rows = pl.ds(pl.multiple_of(c * 2 * m, 2 * m), 2 * m)
        e, s = e_ref[rows], s_ref[rows]
        return grams[0] + dot_t(e, e), grams[1] + dot_t(s, s)

    zero = jnp.zeros((w, w), F32)
    dlocal[...] = diagonal_blocks(*lax.fori_loop(0, CHUNKS // 2, square, (zero, zero)))
    copies = split_sum(place, dlocal, dhalf, dslot, dslots, dresult, send, recv, 0)
    ours = copy(dresult, dother, send.at[17], recv.at[17], across)
    ours.start()

    def take(c, total):
        rows, out = bulk(c)
        out.wait_recv()
        return total + dot_t(e_ref[rows], r_ref[rows])

    product = lax.fori_loop(0, CHUNKS, take, zero)
    clocal[...] = cross_block(product)
    first = copy(clocal, cslot, send.at[18], recv.at[18], (place.other, place.z))
    first.start()
    first.wait_recv()
    csum[...] = clocal[...] + cslot[...]
    more = exchange(place, csum, cslots, send, recv, 19)
    cross = collect(more, cslots, csum[...])
    ours.wait_recv()
    diagonal = jnp.where(low_lanes((h, w), h), dresult[...], dother[...])
    gout_ref[...] = assemble(diagonal, cross)

    def sent(c, _):
        bulk(c)[1].wait_send()
        return 0

    lax.fori_loop(0, CHUNKS, sent, 0)
    for c in copies + [ours, first] + more:
        c.wait_send()


def last_kernel(p_ref, q_ref, g_ref, out_ref, w_ref, both, corr):
    n, w = p_ref.shape
    w_ref[...] = block_form(orthogonalizer(g_ref[...], both, corr))
    h = w // 2
    m = n // CHUNKS
    low = low_lanes((m, w), h)

    def write(c, _):
        rows = pl.ds(pl.multiple_of(c * m, m), m)
        es = dot(jnp.concatenate([p_ref[rows], q_ref[rows]], axis=1), w_ref[...])
        e, s = es[:, :w], es[:, w:]
        out_ref[rows] = jnp.where(low, e, s)
        out_ref[pl.ds(pl.multiple_of(n + c * m, m), m)] = pltpu.roll(jnp.where(low, s, e), h, 1)
        return 0

    lax.fori_loop(0, CHUNKS, write, 0)


def body(matrix, partner):
    rows_here, width = matrix.shape
    n, h, q = rows_here // 2, width // 2, width // 4
    bit_total = lax.axis_size("pair").bit_length() - 1
    my_pair = lax.axis_index("pair")
    vmem = pl.BlockSpec(memory_space=pltpu.VMEM)
    dma = pltpu.SemaphoreType.DMA
    tall = jax.ShapeDtypeStruct((n, width), F32)
    square = jax.ShapeDtypeStruct((width, width), F32)

    def buf(*shape):
        return pltpu.VMEM(shape, F32)

    start = pl.pallas_call(
        start_kernel,
        out_shape=(tall, tall, square),
        in_specs=[vmem],
        out_specs=(vmem, vmem, vmem),
        scratch_shapes=[
            buf(h + q, width), buf((h + q) // 2, width), buf((h + q) // 2, width),
            buf(15, (h + q) // 2, width), buf(h + q, width), dma((17,)), dma((17,)),
        ],
        compiler_params=pltpu.CompilerParams(collective_id=8, has_side_effects=True, vmem_limit_bytes=32 << 20),
        name="start",
    )

    def turn(bit):
        return pl.pallas_call(
            functools.partial(round_kernel, 2**bit),
            out_shape=(tall, tall, square),
            in_specs=[vmem] * 3,
            out_specs=(vmem, vmem, vmem),
            scratch_shapes=[
                buf(n, width), buf(2 * width, 2 * width),
                buf(h, width), buf(q, width), buf(q, width), buf(15, q, width), buf(h, width), buf(h, width),
                buf(q, width), buf(q, width), buf(q, width), buf(15, q, width),
                dma((CHUNKS,)), dma((CHUNKS,)), dma((34,)), dma((34,)), buf(2 * width, width), buf(width, width),
            ],
            compiler_params=pltpu.CompilerParams(collective_id=bit, has_side_effects=True, vmem_limit_bytes=32 << 20),
            name=f"turn{bit}",
        )

    last = pl.pallas_call(
        last_kernel,
        out_shape=jax.ShapeDtypeStruct((rows_here, width), F32),
        in_specs=[vmem] * 3,
        out_specs=vmem,
        scratch_shapes=[buf(2 * width, 2 * width), buf(2 * width, width), buf(width, width)],
        compiler_params=pltpu.CompilerParams(vmem_limit_bytes=32 << 20),
        name="last",
    )

    turns = [turn(bit) for bit in range(bit_total)]
    offsets = jnp.bitwise_xor(partner[:, my_pair], my_pair)
    bits = jnp.sum(
        jnp.stack([(jnp.bitwise_and(jnp.right_shift(offsets, b), 1) * b) for b in range(bit_total)]), axis=0
    )
    state = start(matrix)
    for round_index in range(ROUNDS - 1):
        state = lax.switch(bits[round_index], turns, *state)
    return last(*state)


def solution(mesh):
    in_specs = (P("row", "pair"), P())
    out_specs = P("row", "pair")
    return jax.shard_map(body, mesh=mesh, in_specs=in_specs, out_specs=out_specs, check_vma=False)
```

```python
import functools

import jax
import jax.numpy as jnp
from jax import lax
from jax.experimental import pallas as pl
from jax.experimental.pallas import tpu as pltpu
from jax.sharding import PartitionSpec as P

ROUNDS = 4
NS_ITERS = 6
CHUNKS = 8
STORES = 4
LOADS = 2
MESH = pl.DeviceIdType.MESH
HIGHEST = lax.Precision.HIGHEST
F32 = jnp.float32

OFFSETS = sorted(
    [(dx, dy) for dx in range(4) for dy in range(4) if dx or dy],
    key=lambda d: -(min(d[0], 4 - d[0]) + min(d[1], 4 - d[1])),
)


def dot(a, b):
    return jnp.dot(a, b, precision=HIGHEST, preferred_element_type=F32)


def dot_t(a, b):
    return lax.dot_general(
        a, b, (((0,), (0,)), ((), ())), precision=HIGHEST, preferred_element_type=F32
    )


def low_lanes(shape, half):
    return lax.broadcasted_iota(jnp.int32, shape, 1) < half


def orthogonalizer(gram, pair):
    size = gram.shape[0]
    rows = lax.broadcasted_iota(jnp.int32, (size, size), 0)
    cols = lax.broadcasted_iota(jnp.int32, (size, size), 1)
    identity = jnp.where(rows == cols, 1.0, 0.0).astype(F32)
    square_sum = jnp.sum(jnp.sum(gram * gram, axis=0, keepdims=True), axis=1, keepdims=True)
    frobenius = jnp.sqrt(square_sum)
    root = gram / frobenius
    inverse = 1.5 * identity - 0.5 * root
    pair[0] = dot(root, inverse)
    pair[1] = inverse

    def step(_, carry):
        correction = 1.5 * identity - 0.5 * dot(pair[1], pair[0])
        root, inverse = dot(pair[0], correction), dot(correction, pair[1])
        pair[0] = root
        pair[1] = inverse
        return carry

    lax.fori_loop(0, NS_ITERS - 2, step, 0)
    inverse = dot(1.5 * identity - 0.5 * dot(pair[1], pair[0]), pair[1])
    diagonal = jnp.sum(gram * identity, axis=0, keepdims=True)
    return inverse * (jnp.sqrt(diagonal) / jnp.sqrt(frobenius))


def diagonal_blocks(gram_e, gram_s):
    h = gram_e.shape[0] // 2
    low = low_lanes((h, 2 * h), h)
    a = jnp.where(low, gram_e[:h], gram_e[h:])
    b = jnp.where(low, gram_s[:h], gram_s[h:])
    a = a + pltpu.roll(a, h, 1)
    b = b + pltpu.roll(b, h, 1)
    return jnp.where(low, a, b)


def cross_block(product):
    h = product.shape[0] // 2
    c = jnp.where(low_lanes((h, 2 * h), h), product[h:], product[:h])
    c = c + pltpu.roll(c, h, 1)
    q = h // 2
    return jnp.where(low_lanes((q, 2 * h), h), c[:q], c[q:])


def assemble(diagonal, cross):
    h = diagonal.shape[0]
    low = low_lanes((h, 2 * h), h)
    zero = jnp.zeros((h, 2 * h), F32)
    c = jnp.concatenate([pltpu.roll(cross, h, 1), cross], axis=0)
    upper = jnp.concatenate([jnp.where(low, 0.0, c), zero], axis=0)
    blocks = jnp.concatenate(
        [jnp.where(low, diagonal, 0.0), jnp.where(low, 0.0, diagonal)], axis=0
    )
    return blocks + upper + upper.T


class Place:
    def __init__(self):
        self.row, self.z = lax.axis_index("row"), lax.axis_index("pair")
        self.core = lax.rem(self.row, 2)
        y = lax.rem(lax.div(self.row, 2), 4)
        x = lax.div(self.row, 8)
        self.other = self.row + 1 - 2 * self.core
        self.peers = [
            (lax.rem(x + dx, 4) * 4 + lax.rem(y + dy, 4)) * 2 + self.core for dx, dy in OFFSETS
        ]

    def greet(self, more=()):
        barrier = pltpu.get_barrier_semaphore()
        targets = [(self.row, p) for p in more] + [(r, self.z) for r in self.peers + [self.other]]
        for target in targets:
            pl.semaphore_signal(barrier, inc=1, device_id=target, device_id_type=MESH)
        return lambda: pl.semaphore_wait(barrier, len(targets))

    def half(self, ref_rows):
        h = ref_rows // 2
        return (
            pl.ds(pl.multiple_of(self.core * h, h), h),
            pl.ds(pl.multiple_of((1 - self.core) * h, h), h),
        )


def copy(src, dst, send, recv, target):
    return pltpu.make_async_remote_copy(
        src_ref=src, dst_ref=dst, send_sem=send, recv_sem=recv,
        device_id=target, device_id_type=MESH,
    )


def exchange(place, src, slots, send, recv, base):
    copies = [
        copy(src, slots.at[k], send.at[base + k], recv.at[base + k], (peer, place.z))
        for k, peer in enumerate(place.peers)
    ]
    for c in copies:
        c.start()
    return copies


def collect(copies, slots, total):
    for k in reversed(range(len(copies))):
        copies[k].wait_recv()
        total = total + slots[k]
    return total


class SplitSum:
    def __init__(self, place, local, half, slot, slots, result, send, recv, base):
        self.place, self.slots, self.half, self.result = place, slots, half, result
        self.mine, theirs = place.half(local.shape[0])
        other = (place.other, place.z)
        first = copy(local.at[theirs], slot, send.at[base], recv.at[base], other)
        first.start()
        first.wait_recv()
        half[...] = local[self.mine] + slot[...]
        self.copies = exchange(place, half, slots, send, recv, base + 1)
        rows = result.at[self.mine]
        self.last = copy(rows, rows, send.at[base + 16], recv.at[base + 16], other)
        self.all = [first] + self.copies + [self.last]

    def share(self):
        self.result[self.mine] = collect(self.copies, self.slots, self.half[...])
        self.last.start()

    def finish(self):
        self.last.wait_recv()


def start_kernel(
    x_hbm, partner_ref, e_ref, s_ref, g_ref, bit0_ref, bit1_ref, bit2_ref,
    x_ref, local, half, slot, slots, result, send, recv, load,
):
    n, w = e_ref.shape
    h, m = w // 2, n // LOADS
    loads = [
        [
            pltpu.make_async_copy(x_hbm.at[rows], x_ref.at[rows], load.at[side, c])
            for side, rows in enumerate((pl.ds(c * m, m), pl.ds(n + c * m, m)))
        ]
        for c in range(LOADS)
    ]
    for both in loads:
        for c in both:
            c.start()
    place = Place()
    wait = place.greet()
    for round_index, bit_ref in enumerate((bit0_ref, bit1_ref, bit2_ref)):
        offset = jnp.bitwise_xor(partner_ref[round_index, place.z], place.z)
        bit_ref[0] = sum(jnp.where(offset >= s, 1, 0) for s in (2, 4, 8))
    low = low_lanes((m, w), h)
    ee = ss = es = jnp.zeros((w, w), F32)
    for c in range(LOADS):
        for one in loads[c]:
            one.wait()
        rows = pl.ds(c * m, m)
        top, bottom = x_ref[rows], pltpu.roll(x_ref[pl.ds(n + c * m, m)], h, 1)
        e, s = jnp.where(low, top, bottom), jnp.where(low, bottom, top)
        e_ref[rows] = e
        s_ref[rows] = s
        ee, ss, es = ee + dot_t(e, e), ss + dot_t(s, s), es + dot_t(e, s)
    local[:h] = diagonal_blocks(ee, ss)
    local[h:] = cross_block(es)
    wait()
    total = SplitSum(place, local, half, slot, slots, result, send, recv, 0)
    total.share()
    total.finish()
    g_ref[...] = assemble(result[:h], result[h:])
    for c in total.all:
        c.wait_send()


def block_form(v):
    h = v.shape[0] // 2
    low = low_lanes((h, 2 * h), h)
    va, vb = v[:h], v[h:]
    ra, rb = pltpu.roll(va, h, 1), pltpu.roll(vb, h, 1)
    left = [jnp.where(low, va, 0.0), jnp.where(low, 0.0, ra), jnp.where(low, 0.0, rb), jnp.where(low, vb, 0.0)]
    right = [jnp.where(low, 0.0, va), jnp.where(low, ra, 0.0), jnp.where(low, rb, 0.0), jnp.where(low, 0.0, vb)]
    return jnp.concatenate(
        [jnp.concatenate(left, axis=0), jnp.concatenate(right, axis=0)], axis=1
    )


def round_kernel(
    stride, p_ref, q_ref, g_ref, e_ref, r_ref, gout_ref,
    s_ref, w_ref, dlocal, dhalf, dslot, dslots, dresult, dother, clocal, cslot, csum, cslots,
    bsend, brecv, send, recv, pair,
):
    place = Place()
    bit = lax.rem(lax.div(place.z, stride), 2)
    partner = place.z + stride * (1 - 2 * bit)
    wait = place.greet([partner])
    n, w = p_ref.shape
    h, m = w // 2, n // CHUNKS
    across = (place.row, partner)

    w_ref[...] = block_form(orthogonalizer(g_ref[...], pair))
    wait()

    def bulk(c):
        rows = pl.ds(pl.multiple_of(c * m, m), m)
        return rows, copy(s_ref.at[rows], r_ref.at[rows], bsend.at[c], brecv.at[c], across)

    def give(c, _):
        rows, out = bulk(c)
        es = dot(jnp.concatenate([p_ref[rows], q_ref[rows]], axis=1), w_ref[...])
        s_ref[rows] = es[:, w:]
        out.start()
        e_ref[rows] = es[:, :w]
        return 0

    lax.fori_loop(0, CHUNKS, give, 0)

    def square(c, grams):
        rows = pl.ds(pl.multiple_of(c * m, m), m)
        e, s = e_ref[rows], s_ref[rows]
        return grams[0] + dot_t(e, e), grams[1] + dot_t(s, s)

    def take(c, total):
        rows, out = bulk(c)
        out.wait_recv()
        return total + dot_t(e_ref[rows], r_ref[rows])

    def cross():
        return cross_block(lax.fori_loop(0, CHUNKS, take, zero))

    zero = jnp.zeros((w, w), F32)
    dlocal[...] = diagonal_blocks(*lax.fori_loop(0, CHUNKS, square, (zero, zero)))
    total = SplitSum(place, dlocal, dhalf, dslot, dslots, dresult, send, recv, 0)
    ours = copy(dresult, dother, send.at[17], recv.at[17], across)
    first = copy(clocal, cslot, send.at[18], recv.at[18], (place.other, place.z))
    if stride == 1:
        clocal[...] = cross()
        first.start()
        total.share()
    else:
        total.share()
        total.finish()
        ours.start()
        clocal[...] = cross()
        first.start()
    first.wait_recv()
    csum[...] = clocal[...] + cslot[...]
    more = exchange(place, csum, cslots, send, recv, 19)
    if stride == 1:
        total.finish()
        ours.start()
    summed = collect(more, cslots, csum[...])
    ours.wait_recv()
    diagonal = jnp.where(low_lanes((h, w), h), dresult[...], dother[...])
    gout_ref[...] = assemble(diagonal, summed)

    def sent(c, _):
        bulk(c)[1].wait_send()
        return 0

    lax.fori_loop(0, CHUNKS, sent, 0)
    for c in total.all + [ours, first] + more:
        c.wait_send()


def last_kernel(p_ref, q_ref, g_ref, out_hbm, w_ref, pair, out_ref, store):
    n, w = p_ref.shape
    h, m = w // 2, n // STORES
    w_ref[...] = block_form(orthogonalizer(g_ref[...], pair))
    low = low_lanes((m, w), h)

    def stores(c):
        sides = (pl.ds(pl.multiple_of(side * n + c * m, m), m) for side in range(2))
        return [
            (rows, pltpu.make_async_copy(out_ref.at[rows], out_hbm.at[rows], store.at[side, c]))
            for side, rows in enumerate(sides)
        ]

    def write(c, _):
        rows = pl.ds(pl.multiple_of(c * m, m), m)
        es = dot(jnp.concatenate([p_ref[rows], q_ref[rows]], axis=1), w_ref[...])
        e, s = es[:, :w], es[:, w:]
        (top, to_top), (bottom, to_bottom) = stores(c)
        out_ref[top] = jnp.where(low, e, s)
        to_top.start()
        out_ref[bottom] = pltpu.roll(jnp.where(low, s, e), h, 1)
        to_bottom.start()
        return 0

    lax.fori_loop(0, STORES, write, 0)

    def done(c, _):
        for _, one in stores(c):
            one.wait()
        return 0

    lax.fori_loop(0, STORES, done, 0)


def body(matrix, partner):
    rows_here, width = matrix.shape
    n, h, q = rows_here // 2, width // 2, width // 4
    bit_total = lax.axis_size("pair").bit_length() - 1
    vmem = pl.BlockSpec(memory_space=pltpu.VMEM)
    dma = pltpu.SemaphoreType.DMA
    tall = jax.ShapeDtypeStruct((n, width), F32)
    square = jax.ShapeDtypeStruct((width, width), F32)

    def buf(*shape):
        return pltpu.VMEM(shape, F32)

    bit_shape = jax.ShapeDtypeStruct((1,), jnp.int32)
    smem = pl.BlockSpec(memory_space=pltpu.SMEM)
    hbm = pl.BlockSpec(memory_space=pltpu.HBM)
    part = (h + q) // 2
    start = pl.pallas_call(
        start_kernel,
        out_shape=(tall, tall, square) + (bit_shape,) * 3,
        in_specs=[hbm, smem],
        out_specs=(vmem,) * 3 + (smem,) * 3,
        scratch_shapes=[
            buf(rows_here, width), buf(2 * part, width), buf(part, width), buf(part, width),
            buf(15, part, width), buf(2 * part, width), dma((17,)), dma((17,)), dma((2, LOADS)),
        ],
        compiler_params=pltpu.CompilerParams(collective_id=8, has_side_effects=True, vmem_limit_bytes=61_800_000),
        name="start",
    )

    def turn(bit):
        return pl.pallas_call(
            functools.partial(round_kernel, 2**bit),
            out_shape=(tall, tall, square),
            in_specs=[vmem] * 3,
            out_specs=(vmem, vmem, vmem),
            scratch_shapes=[
                buf(n, width), buf(2 * width, 2 * width),
                buf(h, width), buf(q, width), buf(q, width), buf(15, q, width), buf(h, width), buf(h, width),
                buf(q, width), buf(q, width), buf(q, width), buf(15, q, width),
                dma((CHUNKS,)), dma((CHUNKS,)), dma((34,)), dma((34,)), buf(2, width, width),
            ],
            compiler_params=pltpu.CompilerParams(collective_id=bit, has_side_effects=True, vmem_limit_bytes=32 << 20),
            name=f"turn{bit}",
        )

    last = pl.pallas_call(
        last_kernel,
        out_shape=jax.ShapeDtypeStruct((rows_here, width), F32),
        in_specs=[vmem] * 3,
        out_specs=hbm,
        scratch_shapes=[
            buf(2 * width, 2 * width), buf(2, width, width), buf(rows_here, width), dma((2, STORES)),
        ],
        compiler_params=pltpu.CompilerParams(vmem_limit_bytes=32 << 20),
        name="last",
    )

    turns = [turn(bit) for bit in range(bit_total)]
    *state, bit0, bit1, bit2 = start(matrix, partner)
    for bit in (bit0, bit1, bit2):
        state = lax.switch(bit[0], turns, *state)
    return last(*state)


def solution(mesh):
    in_specs = (P("row", "pair"), P())
    out_specs = P("row", "pair")
    return jax.shard_map(body, mesh=mesh, in_specs=in_specs, out_specs=out_specs, check_vma=False)
```

```python
import functools

import jax
import jax.numpy as jnp
from jax import lax
from jax.experimental import pallas as pl
from jax.experimental.pallas import tpu as pltpu
from jax.sharding import PartitionSpec as P

ROUNDS = 4
NS_ITERS = 6
CHUNKS = 8
STORES = 4
LOADS = 2
MESH = pl.DeviceIdType.MESH
HIGHEST = lax.Precision.HIGHEST
F32 = jnp.float32

OFFSETS = sorted(
    [(dx, dy) for dx in range(4) for dy in range(4) if dx or dy],
    key=lambda d: -(min(d[0], 4 - d[0]) + min(d[1], 4 - d[1])),
)


def dot(a, b):
    return jnp.dot(a, b, precision=HIGHEST, preferred_element_type=F32)


def dot_t(a, b):
    return lax.dot_general(
        a, b, (((0,), (0,)), ((), ())), precision=HIGHEST, preferred_element_type=F32
    )


def low_lanes(shape, half):
    return lax.broadcasted_iota(jnp.int32, shape, 1) < half


def orthogonalizer(gram, pair):
    size = gram.shape[0]
    rows = lax.broadcasted_iota(jnp.int32, (size, size), 0)
    cols = lax.broadcasted_iota(jnp.int32, (size, size), 1)
    identity = jnp.where(rows == cols, 1.0, 0.0).astype(F32)
    square_sum = jnp.sum(jnp.sum(gram * gram, axis=0, keepdims=True), axis=1, keepdims=True)
    frobenius = jnp.sqrt(square_sum)
    root = gram / frobenius
    inverse = 1.5 * identity - 0.5 * root
    pair[0] = dot(root, inverse)
    pair[1] = inverse

    def step(_, carry):
        correction = 1.5 * identity - 0.5 * dot(pair[1], pair[0])
        root, inverse = dot(pair[0], correction), dot(correction, pair[1])
        pair[0] = root
        pair[1] = inverse
        return carry

    lax.fori_loop(0, NS_ITERS - 2, step, 0)
    inverse = dot(1.5 * identity - 0.5 * dot(pair[1], pair[0]), pair[1])
    diagonal = jnp.sum(gram * identity, axis=0, keepdims=True)
    return inverse * (jnp.sqrt(diagonal) / jnp.sqrt(frobenius))


def diagonal_blocks(gram_e, gram_s):
    h = gram_e.shape[0] // 2
    low = low_lanes((h, 2 * h), h)
    a = jnp.where(low, gram_e[:h], gram_e[h:])
    b = jnp.where(low, gram_s[:h], gram_s[h:])
    a = a + pltpu.roll(a, h, 1)
    b = b + pltpu.roll(b, h, 1)
    return jnp.where(low, a, b)


def pack_high(block):
    r, w = block.shape
    low = low_lanes((r // 2, w), w // 2)
    return jnp.where(low, pltpu.roll(block[: r // 2], w // 2, 1), block[r // 2 :])


def unpack_high(packed):
    return jnp.concatenate([pltpu.roll(packed, packed.shape[1] // 2, 1), packed], axis=0)


def cross_block(product):
    h = product.shape[0] // 2
    c = jnp.where(low_lanes((h, 2 * h), h), product[h:], product[:h])
    c = c + pltpu.roll(c, h, 1)
    q = h // 2
    return jnp.where(low_lanes((q, 2 * h), h), c[:q], c[q:])


def assemble(diagonal, cross):
    h = diagonal.shape[0]
    low = low_lanes((h, 2 * h), h)
    zero = jnp.zeros((h, 2 * h), F32)
    c = jnp.concatenate([pltpu.roll(cross, h, 1), cross], axis=0)
    upper = jnp.concatenate([jnp.where(low, 0.0, c), zero], axis=0)
    blocks = jnp.concatenate(
        [jnp.where(low, diagonal, 0.0), jnp.where(low, 0.0, diagonal)], axis=0
    )
    return blocks + upper + upper.T


class Place:
    def __init__(self):
        self.row, self.z = lax.axis_index("row"), lax.axis_index("pair")
        self.core = lax.rem(self.row, 2)
        y = lax.rem(lax.div(self.row, 2), 4)
        x = lax.div(self.row, 8)
        self.other = self.row + 1 - 2 * self.core
        self.peers = [
            (lax.rem(x + dx, 4) * 4 + lax.rem(y + dy, 4)) * 2 + self.core for dx, dy in OFFSETS
        ]

    def greet(self, more=()):
        barrier = pltpu.get_barrier_semaphore()
        targets = [(self.row, p) for p in more] + [(r, self.z) for r in self.peers + [self.other]]
        for target in targets:
            pl.semaphore_signal(barrier, inc=1, device_id=target, device_id_type=MESH)
        return lambda: pl.semaphore_wait(barrier, len(targets))

    def half(self, ref_rows):
        h = ref_rows // 2
        return (
            pl.ds(pl.multiple_of(self.core * h, h), h),
            pl.ds(pl.multiple_of((1 - self.core) * h, h), h),
        )


def copy(src, dst, send, recv, target):
    return pltpu.make_async_remote_copy(
        src_ref=src, dst_ref=dst, send_sem=send, recv_sem=recv,
        device_id=target, device_id_type=MESH,
    )


def exchange(place, src, slots, send, recv, base):
    copies = [
        copy(src, slots.at[k], send.at[base + k], recv.at[base + k], (peer, place.z))
        for k, peer in enumerate(place.peers)
    ]
    for c in copies:
        c.start()
    return copies


def collect(copies, slots, total):
    for k in reversed(range(len(copies))):
        copies[k].wait_recv()
        total = total + slots[k]
    return total


class SplitSum:
    def __init__(self, place, local, half, slot, slots, result, send, recv, base):
        self.place, self.slots, self.half, self.result = place, slots, half, result
        self.mine, theirs = place.half(local.shape[0])
        other = (place.other, place.z)
        first = copy(local.at[theirs], slot, send.at[base], recv.at[base], other)
        first.start()
        first.wait_recv()
        half[...] = local[self.mine] + slot[...]
        self.copies = exchange(place, half, slots, send, recv, base + 1)
        rows = result.at[self.mine]
        self.last = copy(rows, rows, send.at[base + 16], recv.at[base + 16], other)
        self.all = [first] + self.copies + [self.last]

    def share(self):
        self.result[self.mine] = collect(self.copies, self.slots, self.half[...])
        self.last.start()

    def finish(self):
        self.last.wait_recv()


def start_kernel(
    x_hbm, partner_ref, e_ref, s_ref, g_ref, bit0_ref, bit1_ref, bit2_ref,
    x_ref, local, half, slot, slots, result, send, recv, load,
):
    n, w = e_ref.shape
    h, m = w // 2, n // LOADS
    loads = [
        [
            pltpu.make_async_copy(x_hbm.at[rows], x_ref.at[rows], load.at[side, c])
            for side, rows in enumerate((pl.ds(c * m, m), pl.ds(n + c * m, m)))
        ]
        for c in range(LOADS)
    ]
    for both in loads:
        for c in both:
            c.start()
    place = Place()
    wait = place.greet()
    for round_index, bit_ref in enumerate((bit0_ref, bit1_ref, bit2_ref)):
        offset = jnp.bitwise_xor(partner_ref[round_index, place.z], place.z)
        bit_ref[0] = sum(jnp.where(offset >= s, 1, 0) for s in (2, 4, 8))
    low = low_lanes((m, w), h)
    ee = ss = es = jnp.zeros((w, w), F32)
    for c in range(LOADS):
        for one in loads[c]:
            one.wait()
        rows = pl.ds(c * m, m)
        top, bottom = x_ref[rows], pltpu.roll(x_ref[pl.ds(n + c * m, m)], h, 1)
        e, s = jnp.where(low, top, bottom), jnp.where(low, bottom, top)
        e_ref[rows] = e
        s_ref[rows] = s
        ee, ss, es = ee + dot_t(e, e), ss + dot_t(s, s), es + dot_t(e, s)
    local[:h] = diagonal_blocks(ee, ss)
    local[h:] = cross_block(es)
    wait()
    total = SplitSum(place, local, half, slot, slots, result, send, recv, 0)
    total.share()
    total.finish()
    g_ref[...] = assemble(result[:h], result[h:])
    for c in total.all:
        c.wait_send()


def block_form(v):
    h = v.shape[0] // 2
    low = low_lanes((h, 2 * h), h)
    va, vb = v[:h], v[h:]
    ra, rb = pltpu.roll(va, h, 1), pltpu.roll(vb, h, 1)
    left = [jnp.where(low, va, 0.0), jnp.where(low, 0.0, ra), jnp.where(low, 0.0, rb), jnp.where(low, vb, 0.0)]
    right = [jnp.where(low, 0.0, va), jnp.where(low, ra, 0.0), jnp.where(low, rb, 0.0), jnp.where(low, 0.0, vb)]
    return jnp.concatenate(
        [jnp.concatenate(left, axis=0), jnp.concatenate(right, axis=0)], axis=1
    )


def round_kernel(
    stride, p_ref, q_ref, g_ref, e_ref, r_ref, gout_ref,
    s_ref, w_ref, dlocal, dhalf, dslot, dslots, dresult, bhalf, bother, clocal, cslot, csum, cslots,
    bsend, brecv, send, recv, pair,
):
    place = Place()
    bit = lax.rem(lax.div(place.z, stride), 2)
    partner = place.z + stride * (1 - 2 * bit)
    wait = place.greet([partner])
    n, w = p_ref.shape
    h, m = w // 2, n // CHUNKS
    across = (place.row, partner)

    w_ref[...] = block_form(orthogonalizer(g_ref[...], pair))
    wait()

    def bulk(c):
        rows = pl.ds(pl.multiple_of(c * m, m), m)
        return rows, copy(s_ref.at[rows], r_ref.at[rows], bsend.at[c], brecv.at[c], across)

    def give(c, _):
        rows, out = bulk(c)
        es = dot(jnp.concatenate([p_ref[rows], q_ref[rows]], axis=1), w_ref[...])
        s_ref[rows] = es[:, w:]
        out.start()
        e_ref[rows] = es[:, :w]
        return 0

    lax.fori_loop(0, CHUNKS, give, 0)

    def square(c, grams):
        rows = pl.ds(pl.multiple_of(c * m, m), m)
        e, s = e_ref[rows], s_ref[rows]
        return grams[0] + dot_t(e, e), grams[1] + dot_t(s, s)

    def take(c, total):
        rows, out = bulk(c)
        out.wait_recv()
        return total + dot_t(e_ref[rows], r_ref[rows])

    def cross():
        return cross_block(lax.fori_loop(0, CHUNKS, take, zero))

    zero = jnp.zeros((w, w), F32)
    dlocal[...] = diagonal_blocks(*lax.fori_loop(0, CHUNKS, square, (zero, zero)))
    total = SplitSum(place, dlocal, dhalf, dslot, dslots, dresult, send, recv, 0)
    mine, _ = place.half(bother.shape[0])
    other = (place.other, place.z)
    ours = copy(bhalf, bother.at[mine], send.at[17], recv.at[17], across)
    spread = copy(bother.at[mine], bother.at[mine], send.at[34], recv.at[34], other)

    def give_diagonal():
        total.share()
        bhalf[...] = pack_high(dresult[total.mine])
        ours.start()

    first = copy(clocal, cslot, send.at[18], recv.at[18], other)
    if stride == 1:
        clocal[...] = cross()
        first.start()
        give_diagonal()
    else:
        give_diagonal()
        clocal[...] = cross()
        first.start()
    first.wait_recv()
    csum[...] = clocal[...] + cslot[...]
    more = exchange(place, csum, cslots, send, recv, 19)
    total.finish()
    ours.wait_recv()
    spread.start()
    summed = collect(more, cslots, csum[...])
    spread.wait_recv()
    q = h // 4
    theirs = jnp.concatenate([unpack_high(bother[:q]), unpack_high(bother[q:])], axis=0)
    diagonal = jnp.where(low_lanes((h, w), h), dresult[...], theirs)
    gout_ref[...] = assemble(diagonal, summed)

    def sent(c, _):
        bulk(c)[1].wait_send()
        return 0

    lax.fori_loop(0, CHUNKS, sent, 0)
    for c in total.all + [ours, spread, first] + more:
        c.wait_send()


def last_kernel(p_ref, q_ref, g_ref, out_hbm, w_ref, pair, out_ref, store):
    n, w = p_ref.shape
    h, m = w // 2, n // STORES
    w_ref[...] = block_form(orthogonalizer(g_ref[...], pair))
    low = low_lanes((m, w), h)

    def stores(c):
        sides = (pl.ds(pl.multiple_of(side * n + c * m, m), m) for side in range(2))
        return [
            (rows, pltpu.make_async_copy(out_ref.at[rows], out_hbm.at[rows], store.at[side, c]))
            for side, rows in enumerate(sides)
        ]

    def write(c, _):
        rows = pl.ds(pl.multiple_of(c * m, m), m)
        es = dot(jnp.concatenate([p_ref[rows], q_ref[rows]], axis=1), w_ref[...])
        e, s = es[:, :w], es[:, w:]
        (top, to_top), (bottom, to_bottom) = stores(c)
        out_ref[top] = jnp.where(low, e, s)
        to_top.start()
        out_ref[bottom] = pltpu.roll(jnp.where(low, s, e), h, 1)
        to_bottom.start()
        return 0

    lax.fori_loop(0, STORES, write, 0)

    def done(c, _):
        for _, one in stores(c):
            one.wait()
        return 0

    lax.fori_loop(0, STORES, done, 0)


def body(matrix, partner):
    rows_here, width = matrix.shape
    n, h, q = rows_here // 2, width // 2, width // 4
    bit_total = lax.axis_size("pair").bit_length() - 1
    vmem = pl.BlockSpec(memory_space=pltpu.VMEM)
    dma = pltpu.SemaphoreType.DMA
    tall = jax.ShapeDtypeStruct((n, width), F32)
    square = jax.ShapeDtypeStruct((width, width), F32)

    def buf(*shape):
        return pltpu.VMEM(shape, F32)

    bit_shape = jax.ShapeDtypeStruct((1,), jnp.int32)
    smem = pl.BlockSpec(memory_space=pltpu.SMEM)
    hbm = pl.BlockSpec(memory_space=pltpu.HBM)
    part = (h + q) // 2
    start = pl.pallas_call(
        start_kernel,
        out_shape=(tall, tall, square) + (bit_shape,) * 3,
        in_specs=[hbm, smem],
        out_specs=(vmem,) * 3 + (smem,) * 3,
        scratch_shapes=[
            buf(rows_here, width), buf(2 * part, width), buf(part, width), buf(part, width),
            buf(15, part, width), buf(2 * part, width), dma((17,)), dma((17,)), dma((2, LOADS)),
        ],
        compiler_params=pltpu.CompilerParams(collective_id=8, has_side_effects=True, vmem_limit_bytes=61_800_000),
        name="start",
    )

    def turn(bit):
        return pl.pallas_call(
            functools.partial(round_kernel, 2**bit),
            out_shape=(tall, tall, square),
            in_specs=[vmem] * 3,
            out_specs=(vmem, vmem, vmem),
            scratch_shapes=[
                buf(n, width), buf(2 * width, 2 * width),
                buf(h, width), buf(q, width), buf(q, width), buf(15, q, width), buf(h, width), buf(q // 2, width), buf(q, width),
                buf(q, width), buf(q, width), buf(q, width), buf(15, q, width),
                dma((CHUNKS,)), dma((CHUNKS,)), dma((35,)), dma((35,)), buf(2, width, width),
            ],
            compiler_params=pltpu.CompilerParams(collective_id=bit, has_side_effects=True, vmem_limit_bytes=32 << 20),
            name=f"turn{bit}",
        )

    last = pl.pallas_call(
        last_kernel,
        out_shape=jax.ShapeDtypeStruct((rows_here, width), F32),
        in_specs=[vmem] * 3,
        out_specs=hbm,
        scratch_shapes=[
            buf(2 * width, 2 * width), buf(2, width, width), buf(rows_here, width), dma((2, STORES)),
        ],
        compiler_params=pltpu.CompilerParams(vmem_limit_bytes=32 << 20),
        name="last",
    )

    turns = [turn(bit) for bit in range(bit_total)]
    *state, bit0, bit1, bit2 = start(matrix, partner)
    for bit in (bit0, bit1, bit2):
        state = lax.switch(bit[0], turns, *state)
    return last(*state)


def solution(mesh):
    in_specs = (P("row", "pair"), P())
    out_specs = P("row", "pair")
    return jax.shard_map(body, mesh=mesh, in_specs=in_specs, out_specs=out_specs, check_vma=False)
```

```python
import functools

import jax
import jax.numpy as jnp
from jax import lax
from jax.experimental import pallas as pl
from jax.experimental.pallas import tpu as pltpu
from jax.sharding import PartitionSpec as P

ROUNDS = 4
NS_ITERS = 6
CHUNKS = 8
STORES = 4
LOADS = 4
SKIPS = (3, 2, 1, 1)
MESH = pl.DeviceIdType.MESH
HIGHEST = lax.Precision.HIGHEST
F32 = jnp.float32

OFFSETS = sorted(
    [(dx, dy) for dx in range(4) for dy in range(4) if dx or dy],
    key=lambda d: -(min(d[0], 4 - d[0]) + min(d[1], 4 - d[1])),
)


def dot(a, b):
    return jnp.dot(a, b, precision=HIGHEST, preferred_element_type=F32)


def dot_t(a, b):
    return lax.dot_general(
        a, b, (((0,), (0,)), ((), ())), precision=HIGHEST, preferred_element_type=F32
    )


def low_lanes(shape, half):
    return lax.broadcasted_iota(jnp.int32, shape, 1) < half


def orthogonalizer(gram, pair):
    size = gram.shape[0]
    rows = lax.broadcasted_iota(jnp.int32, (size, size), 0)
    cols = lax.broadcasted_iota(jnp.int32, (size, size), 1)
    identity = jnp.where(rows == cols, 1.0, 0.0).astype(F32)
    square_sum = jnp.sum(jnp.sum(gram * gram, axis=0, keepdims=True), axis=1, keepdims=True)
    frobenius = jnp.sqrt(square_sum)
    root = gram / frobenius
    inverse = 1.5 * identity - 0.5 * root
    pair[0] = dot(root, inverse)
    pair[1] = inverse

    def step(_, carry):
        correction = 1.5 * identity - 0.5 * dot(pair[1], pair[0])
        root, inverse = dot(pair[0], correction), dot(correction, pair[1])
        pair[0] = root
        pair[1] = inverse
        return carry

    lax.fori_loop(0, NS_ITERS - 2, step, 0)
    inverse = dot(1.5 * identity - 0.5 * dot(pair[1], pair[0]), pair[1])
    diagonal = jnp.sum(gram * identity, axis=0, keepdims=True)
    return inverse * (jnp.sqrt(diagonal) / jnp.sqrt(frobenius))


def diagonal_blocks(gram_e, gram_s):
    h = gram_e.shape[0] // 2
    low = low_lanes((h, 2 * h), h)
    a = jnp.where(low, gram_e[:h], gram_e[h:])
    b = jnp.where(low, gram_s[:h], gram_s[h:])
    a = a + pltpu.roll(a, h, 1)
    b = b + pltpu.roll(b, h, 1)
    return jnp.where(low, a, b)


def pack_high(block):
    r, w = block.shape
    low = low_lanes((r // 2, w), w // 2)
    return jnp.where(low, pltpu.roll(block[: r // 2], w // 2, 1), block[r // 2 :])


def unpack_high(packed):
    return jnp.concatenate([pltpu.roll(packed, packed.shape[1] // 2, 1), packed], axis=0)


def cross_block(product):
    h = product.shape[0] // 2
    c = jnp.where(low_lanes((h, 2 * h), h), product[h:], product[:h])
    c = c + pltpu.roll(c, h, 1)
    q = h // 2
    return jnp.where(low_lanes((q, 2 * h), h), c[:q], c[q:])


def assemble(diagonal, cross):
    h = diagonal.shape[0]
    low = low_lanes((h, 2 * h), h)
    zero = jnp.zeros((h, 2 * h), F32)
    c = jnp.concatenate([pltpu.roll(cross, h, 1), cross], axis=0)
    upper = jnp.concatenate([jnp.where(low, 0.0, c), zero], axis=0)
    blocks = jnp.concatenate(
        [jnp.where(low, diagonal, 0.0), jnp.where(low, 0.0, diagonal)], axis=0
    )
    return blocks + upper + upper.T


class Place:
    def __init__(self):
        self.row, self.z = lax.axis_index("row"), lax.axis_index("pair")
        self.core = lax.rem(self.row, 2)
        y = lax.rem(lax.div(self.row, 2), 4)
        x = lax.div(self.row, 8)
        self.other = self.row + 1 - 2 * self.core
        self.peers = [
            (lax.rem(x + dx, 4) * 4 + lax.rem(y + dy, 4)) * 2 + self.core for dx, dy in OFFSETS
        ]

    def greet(self, more=()):
        barrier = pltpu.get_barrier_semaphore()
        targets = [(self.row, p) for p in more] + [(r, self.z) for r in self.peers + [self.other]]
        for target in targets:
            pl.semaphore_signal(barrier, inc=1, device_id=target, device_id_type=MESH)
        return lambda: pl.semaphore_wait(barrier, len(targets))

    def half(self, ref_rows):
        h = ref_rows // 2
        return (
            pl.ds(pl.multiple_of(self.core * h, h), h),
            pl.ds(pl.multiple_of((1 - self.core) * h, h), h),
        )


def copy(src, dst, send, recv, target):
    return pltpu.make_async_remote_copy(
        src_ref=src, dst_ref=dst, send_sem=send, recv_sem=recv,
        device_id=target, device_id_type=MESH,
    )


def exchange(place, src, slots, send, recv, base):
    copies = [
        copy(src, slots.at[k], send.at[base + k], recv.at[base + k], (peer, place.z))
        for k, peer in enumerate(place.peers)
    ]
    for c in copies:
        c.start()
    return copies


def collect(copies, slots, total):
    for k in reversed(range(len(copies))):
        copies[k].wait_recv()
        total = total + slots[k]
    return total


class SplitSum:
    def __init__(self, place, local, half, slot, slots, result, send, recv, base):
        self.place, self.slots, self.half, self.result = place, slots, half, result
        self.mine, theirs = place.half(local.shape[0])
        other = (place.other, place.z)
        first = copy(local.at[theirs], slot, send.at[base], recv.at[base], other)
        first.start()
        first.wait_recv()
        half[...] = local[self.mine] + slot[...]
        self.copies = exchange(place, half, slots, send, recv, base + 1)
        rows = result.at[self.mine]
        self.last = copy(rows, rows, send.at[base + 16], recv.at[base + 16], other)
        self.all = [first] + self.copies + [self.last]

    def share(self):
        self.result[self.mine] = collect(self.copies, self.slots, self.half[...])
        self.last.start()

    def finish(self):
        self.last.wait_recv()


def block_form(v):
    h = v.shape[0] // 2
    low = low_lanes((h, 2 * h), h)
    va, vb = v[:h], v[h:]
    ra, rb = pltpu.roll(va, h, 1), pltpu.roll(vb, h, 1)
    left = [jnp.where(low, va, 0.0), jnp.where(low, 0.0, ra), jnp.where(low, 0.0, rb), jnp.where(low, vb, 0.0)]
    right = [jnp.where(low, 0.0, va), jnp.where(low, ra, 0.0), jnp.where(low, rb, 0.0), jnp.where(low, 0.0, vb)]
    return jnp.concatenate(
        [jnp.concatenate(left, axis=0), jnp.concatenate(right, axis=0)], axis=1
    )


def right_form(v):
    h = v.shape[0] // 2
    low = low_lanes((h, 2 * h), h)
    va, vb = v[:h], v[h:]
    ra, rb = pltpu.roll(va, h, 1), pltpu.roll(vb, h, 1)
    return jnp.concatenate(
        [jnp.where(low, 0.0, va), jnp.where(low, ra, 0.0), jnp.where(low, rb, 0.0), jnp.where(low, 0.0, vb)],
        axis=0,
    )


def across_from(place, stride):
    bit = lax.rem(lax.div(place.z, stride), 2)
    return place.z + stride * (1 - 2 * bit)


def swap_and_sum(
    stride, place, skip, early, p_ref, q_ref, e_ref, r_ref, gout_ref,
    s_ref, w_ref, dlocal, dhalf, dslot, dslots, dresult, bhalf, bother, clocal, cslot, csum, cslots,
    bsend, brecv, send, recv,
):
    n, w = p_ref.shape
    h, m = w // 2, n // CHUNKS
    across = (place.row, across_from(place, stride))

    def bulk(c):
        rows = pl.ds(pl.multiple_of(c * m, m), m)
        return rows, copy(s_ref.at[rows], r_ref.at[rows], bsend.at[c], brecv.at[c], across)

    def multiply(c, _):
        rows, out = bulk(c)
        es = dot(jnp.concatenate([p_ref[rows], q_ref[rows]], axis=1), w_ref[...])
        s_ref[rows] = es[:, w:]
        pl.when(c >= skip)(out.start)
        e_ref[rows] = es[:, :w]

    def give(k, _):
        multiply(CHUNKS - 1 - k, 0)
        return 0

    lax.fori_loop(0, CHUNKS, give, 0)

    def square(c, grams):
        rows = pl.ds(pl.multiple_of(c * m, m), m)
        e, s = e_ref[rows], s_ref[rows]
        return grams[0] + dot_t(e, e), grams[1] + dot_t(s, s)

    def add(rows, total):
        return total + dot_t(e_ref[rows], r_ref[rows])

    def take(k, total):
        rows, out = bulk(CHUNKS - 1 - k)
        out.wait_recv()
        return add(rows, total)

    def cross():
        total = zero
        if early is not None:
            early[0]()

            def take_early(c, total):
                rows = pl.ds(pl.multiple_of(c * m, m), m)
                r_ref[rows] = early[1](rows)
                return add(rows, total)

            total = lax.fori_loop(0, skip, take_early, total)
        return cross_block(lax.fori_loop(0, CHUNKS - skip, take, total))

    zero = jnp.zeros((w, w), F32)
    dlocal[...] = diagonal_blocks(*lax.fori_loop(0, CHUNKS, square, (zero, zero)))
    total = SplitSum(place, dlocal, dhalf, dslot, dslots, dresult, send, recv, 0)
    mine, _ = place.half(bother.shape[0])
    other = (place.other, place.z)
    ours = copy(bhalf, bother.at[mine], send.at[17], recv.at[17], across)
    spread = copy(bother.at[mine], bother.at[mine], send.at[34], recv.at[34], other)

    def give_diagonal():
        total.share()
        bhalf[...] = pack_high(dresult[total.mine])
        ours.start()

    first = copy(clocal, cslot, send.at[18], recv.at[18], other)
    if stride == 1:
        clocal[...] = cross()
        first.start()
        give_diagonal()
    else:
        give_diagonal()
        clocal[...] = cross()
        first.start()
    first.wait_recv()
    csum[...] = clocal[...] + cslot[...]
    more = exchange(place, csum, cslots, send, recv, 19)
    total.finish()
    ours.wait_recv()
    spread.start()
    summed = collect(more, cslots, csum[...])
    spread.wait_recv()
    q = h // 4
    theirs = jnp.concatenate([unpack_high(bother[:q]), unpack_high(bother[q:])], axis=0)
    diagonal = jnp.where(low_lanes((h, w), h), dresult[...], theirs)
    gout_ref[...] = assemble(diagonal, summed)

    def sent(c, _):
        bulk(c)[1].wait_send()
        return 0

    lax.fori_loop(skip, CHUNKS, sent, 0)
    for c in total.all + [ours, spread, first] + more:
        c.wait_send()


def round_kernel(stride, p_ref, q_ref, g_ref, e_ref, r_ref, gout_ref, pair, s_ref, w_ref, *scratch):
    place = Place()
    wait = place.greet([across_from(place, stride)])
    w_ref[...] = block_form(orthogonalizer(g_ref[...], pair))
    wait()
    swap_and_sum(stride, place, 0, None, p_ref, q_ref, e_ref, r_ref, gout_ref, s_ref, w_ref, *scratch)


def first_kernel(
    stride, skip, x_hbm, e_ref, r_ref, gout_ref,
    x_ref, p_ref, q_ref, raw_p, raw_q, v_ref, v_slot, form_ref, local, half, slot, slots, result, gsend, grecv, load,
    pair, s_ref, w_ref, *scratch,
):
    n, w = e_ref.shape
    h, m = w // 2, n // LOADS

    def loads(c):
        sides = (pl.ds(pl.multiple_of(side * n + c * m, m), m) for side in range(2))
        return [
            pltpu.make_async_copy(x_hbm.at[rows], x_ref.at[rows], load.at[side, c])
            for side, rows in enumerate(sides)
        ]

    for c in range(LOADS):
        for one in loads(c):
            one.start()
    place = Place()
    across = (place.row, across_from(place, stride))
    other = (place.other, place.z)
    wait = place.greet([across[1]])
    low = low_lanes((m, w), h)

    def square(c, grams):
        for one in loads(c):
            one.wait()
        rows = pl.ds(pl.multiple_of(c * m, m), m)
        bottom = pltpu.roll(x_ref[pl.ds(pl.multiple_of(n + c * m, m), m)], h, 1)
        e, s = jnp.where(low, x_ref[rows], bottom), jnp.where(low, bottom, x_ref[rows])
        p_ref[rows] = e
        q_ref[rows] = s
        return grams[0] + dot_t(e, e), grams[1] + dot_t(s, s), grams[2] + dot_t(e, s)

    zero = jnp.zeros((w, w), F32)
    ee, ss, es = lax.fori_loop(0, LOADS, square, (zero, zero, zero))
    local[:h] = diagonal_blocks(ee, ss)
    local[h:] = cross_block(es)
    wait()
    total = SplitSum(place, local, half, slot, slots, result, gsend, grecv, 0)
    raw = pl.ds(0, raw_p.shape[0])
    raws = [
        copy(p_ref.at[raw], raw_p, gsend.at[17], grecv.at[17], across),
        copy(q_ref.at[raw], raw_q, gsend.at[18], grecv.at[18], across),
    ]
    for c in raws:
        c.start()
    total.share()
    total.finish()
    v = orthogonalizer(assemble(result[:h], result[h:]), pair)
    v_ref[...] = pack_high(v)
    mine, _ = place.half(h)
    values = copy(v_ref.at[mine], v_slot.at[mine], gsend.at[19], grecv.at[19], across)
    values.start()
    share = copy(v_slot.at[mine], v_slot.at[mine], gsend.at[20], grecv.at[20], other)
    w_ref[...] = block_form(v)

    def early():
        values.wait_recv()
        share.start()
        for c in raws:
            c.wait_recv()
        share.wait_recv()
        form_ref[...] = right_form(unpack_high(v_slot[...]))

    def early_rows(rows):
        return dot(jnp.concatenate([raw_p[rows], raw_q[rows]], axis=1), form_ref[...])

    swap_and_sum(stride, place, skip, (early, early_rows), p_ref, q_ref, e_ref, r_ref, gout_ref, s_ref, w_ref, *scratch)
    for c in total.all + raws + [values, share]:
        c.wait_send()


def last_kernel(p_ref, q_ref, g_ref, out_hbm, w_ref, pair, out_ref, store):
    n, w = p_ref.shape
    h, m = w // 2, n // STORES
    w_ref[...] = block_form(orthogonalizer(g_ref[...], pair))
    low = low_lanes((m, w), h)

    def stores(c):
        sides = (pl.ds(pl.multiple_of(side * n + c * m, m), m) for side in range(2))
        return [
            (rows, pltpu.make_async_copy(out_ref.at[rows], out_hbm.at[rows], store.at[side, c]))
            for side, rows in enumerate(sides)
        ]

    def write(c, _):
        rows = pl.ds(pl.multiple_of(c * m, m), m)
        es = dot(jnp.concatenate([p_ref[rows], q_ref[rows]], axis=1), w_ref[...])
        e, s = es[:, :w], es[:, w:]
        (top, to_top), (bottom, to_bottom) = stores(c)
        out_ref[top] = jnp.where(low, e, s)
        to_top.start()
        out_ref[bottom] = pltpu.roll(jnp.where(low, s, e), h, 1)
        to_bottom.start()
        return 0

    lax.fori_loop(0, STORES, write, 0)

    def done(c, _):
        for _, one in stores(c):
            one.wait()
        return 0

    lax.fori_loop(0, STORES, done, 0)


def body(matrix, partner):
    rows_here, width = matrix.shape
    n, h, q = rows_here // 2, width // 2, width // 4
    bit_total = lax.axis_size("pair").bit_length() - 1
    vmem = pl.BlockSpec(memory_space=pltpu.VMEM)
    dma = pltpu.SemaphoreType.DMA
    tall = jax.ShapeDtypeStruct((n, width), F32)
    square = jax.ShapeDtypeStruct((width, width), F32)

    def buf(*shape):
        return pltpu.VMEM(shape, F32)

    hbm = pl.BlockSpec(memory_space=pltpu.HBM)
    part = (h + q) // 2

    def common():
        return [
            buf(2, width, width), buf(n, width), buf(2 * width, 2 * width),
            buf(h, width), buf(q, width), buf(q, width), buf(15, q, width), buf(h, width), buf(q // 2, width), buf(q, width),
            buf(q, width), buf(q, width), buf(q, width), buf(15, q, width),
            dma((CHUNKS,)), dma((CHUNKS,)), dma((35,)), dma((35,)),
        ]

    def first(bit):
        skip = SKIPS[bit]
        rows = skip * (n // CHUNKS)
        return pl.pallas_call(
            functools.partial(first_kernel, 2**bit, skip),
            out_shape=(tall, tall, square),
            in_specs=[hbm],
            out_specs=(vmem,) * 3,
            scratch_shapes=[
                buf(rows_here, width), buf(n, width), buf(n, width), buf(rows, width), buf(rows, width),
                buf(h, width), buf(h, width), buf(2 * width, width),
                buf(2 * part, width), buf(part, width), buf(part, width),
                buf(15, part, width), buf(2 * part, width), dma((21,)), dma((21,)), dma((2, LOADS)),
            ] + common(),
            compiler_params=pltpu.CompilerParams(collective_id=8 + bit, has_side_effects=True, vmem_limit_bytes=61_800_000),
            name=f"first{bit}",
        )

    def turn(bit):
        return pl.pallas_call(
            functools.partial(round_kernel, 2**bit),
            out_shape=(tall, tall, square),
            in_specs=[vmem] * 3,
            out_specs=(vmem, vmem, vmem),
            scratch_shapes=common(),
            compiler_params=pltpu.CompilerParams(collective_id=bit, has_side_effects=True, vmem_limit_bytes=32 << 20),
            name=f"turn{bit}",
        )

    last = pl.pallas_call(
        last_kernel,
        out_shape=jax.ShapeDtypeStruct((rows_here, width), F32),
        in_specs=[vmem] * 3,
        out_specs=hbm,
        scratch_shapes=[
            buf(2 * width, 2 * width), buf(2, width, width), buf(rows_here, width), dma((2, STORES)),
        ],
        compiler_params=pltpu.CompilerParams(vmem_limit_bytes=32 << 20),
        name="last",
    )

    turns = [turn(bit) for bit in range(bit_total)]
    my_pair = lax.axis_index("pair")
    offsets = jnp.bitwise_xor(partner[:, my_pair], my_pair)
    bits = jnp.sum(
        jnp.stack([jnp.where(offsets >= 2**b, 1, 0) for b in range(1, bit_total)]), axis=0
    )
    state = lax.switch(bits[0], [first(bit) for bit in range(bit_total)], matrix)
    for round_index in range(1, ROUNDS - 1):
        state = lax.switch(bits[round_index], turns, *state)
    return last(*state)


def solution(mesh):
    in_specs = (P("row", "pair"), P())
    out_specs = P("row", "pair")
    return jax.shard_map(body, mesh=mesh, in_specs=in_specs, out_specs=out_specs, check_vma=False)
```
